256 devices in a mesh: tm: 16 (over z, core), space: 16 (over x, y).
Axes of the slice: x: 4, y: 4, z: 8, core: 2. Of those that a mesh axis runs over, the one named last changes fastest.
Arguments:
- events: bfloat16 [256, 16, 256, 256], P('tm', 'space'), may hold values from -6 to 6
- mix_weight: float32 [9, 256], replicated, may hold values from -1.8 to 1.8
- gain_in: float32 [256], replicated, may hold values from 0.25 to 1.75
- in_weight: bfloat16 [256, 256], replicated, may hold values from -0.375 to 0.375
- out_weight: bfloat16 [256, 256], replicated, may hold values from -0.375 to 0.375
- skip_gain: float32 [256], replicated, may hold values from 0.5 to 1.5
- feedforward_norm_gain: float32 [256], replicated, may hold values from 0.25 to 1.75
- gate_weight: bfloat16 [256, 1024], replicated, may hold values from -0.375 to 0.375
- up_weight: bfloat16 [256, 1024], replicated, may hold values from -0.375 to 0.375
- down_weight: bfloat16 [1024, 256], replicated, may hold values from -0.1875 to 0.1875
- decay: float32 [256, 256], replicated, may hold values from 0.45 to 0.99995, as said below
Outputs:
- layer_out: bfloat16 [256, 16, 256, 256], P('tm', 'space')
The draws below stay inside these ranges and needn't reach their ends.
Inputs may be any that keep to these rules, and one draw needn't show every extreme that they name: Every decay lies strictly between 0 and 1.
All inputs are finite; a program needn't handle non-finite values.
Results may differ from the reference program's by a relative error of at most 0.008.
Values may be sent and summed in bfloat16 or wider, within the bound.
No kernel may reach another device: no remote copies, remote signals or barrier semaphores. Data moves between devices by JAX's collectives and lax.ppermute only.
A program may use at most 128 MiB of HBM per device.

```python
import math
import jax
import jax.numpy as jnp
from jax import lax

D = 256
NS = 256
FFH = 1024
BH = 16
BW = 16
BCOLS = 4
COUNT_TIME_SLOTS = 256
BLOCKS = 16
TOK = 256


def draw_decay(key, part):
    stochastic_seeds = jax.random.split(jax.random.fold_in(key, 17), 6)
    quick = jax.random.bernoulli(stochastic_seeds[0], 0.5, (NS,))
    quick_gap = jax.random.uniform(stochastic_seeds[1], (NS,), jnp.float32, 0.02, 0.033)
    slow_gap = jnp.exp(jax.random.uniform(stochastic_seeds[2], (NS,), jnp.float32, math.log(0.0001), math.log(0.001)))
    base_gap = jnp.where(quick, quick_gap, slow_gap)
    jitter = jnp.exp(jax.random.uniform(stochastic_seeds[3], (COUNT_TIME_SLOTS, NS), jnp.float32, -0.69, 0.69))
    forgetting_speeds = 1.0 - base_gap[None] * jitter
    spike_cluster = jax.random.bernoulli(stochastic_seeds[4], 3.0 / COUNT_TIME_SLOTS, (COUNT_TIME_SLOTS, 1))
    kept_proportion = jax.random.uniform(stochastic_seeds[5], (COUNT_TIME_SLOTS, NS), jnp.float32, 0.5, 0.8)
    forgetting_speeds = jnp.where(spike_cluster, forgetting_speeds * kept_proportion, forgetting_speeds)
    return forgetting_speeds.astype(jnp.float32)


def block_levels(key, dims, shards, smallest, high):
    level, own = 1.0, jax.random.fold_in(key, 6)
    for dim, parts in shards:
        steps = jnp.exp(jax.random.uniform(jax.random.fold_in(own, dim), (parts,), jnp.float32, smallest / len(shards), high / len(shards)))
        level = level * jnp.repeat(steps, dims[dim] // parts).reshape([-1 if axis == dim else 1 for axis in range(len(dims))])
    return level


def scatter_about(own_key, dims, scale, bound, pieces=(), kind=jnp.bfloat16):
    loudness = block_levels(own_key, dims, pieces, -0.22, 0.18) if pieces else 1.0
    values = jax.random.normal(own_key, dims, jnp.float32) * scale * loudness
    return jnp.minimum(jnp.maximum(values, -bound), bound).astype(kind)


def setup_inputs(seed: int = 0) -> dict:
    key_of = jax.random.split(jax.random.key(seed), 12)
    return {
        "events": scatter_about(key_of[0], (COUNT_TIME_SLOTS, BLOCKS, TOK, D), 1.0, 6.0, ((0, 16), (1, 16))),
        "mix_weight": scatter_about(key_of[1], (9, D), 0.3, 1.8, (), jnp.float32),
        "gain_in": jnp.clip(1.0 + 0.15 * jax.random.normal(key_of[2], (D,), jnp.float32), 0.25, 1.75),
        "in_weight": scatter_about(key_of[3], (D, NS), D ** -0.5, 0.375),
        "out_weight": scatter_about(key_of[4], (NS, D), NS ** -0.5, 0.375),
        "skip_gain": jnp.clip(jax.random.uniform(key_of[5], (D,), jnp.float32, 0.5, 1.5), 0.5, 1.5),
        "feedforward_norm_gain": jnp.clip(1.0 + 0.15 * jax.random.normal(key_of[6], (D,), jnp.float32), 0.25, 1.75),
        "gate_weight": scatter_about(key_of[7], (D, FFH), D ** -0.5, 0.375),
        "up_weight": scatter_about(key_of[8], (D, FFH), D ** -0.5, 0.375),
        "down_weight": scatter_about(key_of[9], (FFH, D), FFH ** -0.5, 0.1875),
        "decay": draw_decay(jax.random.fold_in(key_of[11], 71), 0),
    }


def rms_norm(values, gain):
    scale = lax.rsqrt(lax.optimization_barrier(jnp.mean(values * values, axis=-1, keepdims=True)) + 1e-05)
    return (values * scale * gain).astype(jnp.bfloat16)

def reference(events, mix_weight, gain_in, in_weight, out_weight, skip_gain, feedforward_norm_gain, gate_weight, up_weight, down_weight, decay):
    lattice_lines = BLOCKS // BCOLS
    offset_blocks = BCOLS // 2

    def to_map(frame):
        placed = jnp.roll(frame, offset_blocks, axis=0)
        return placed.reshape(lattice_lines, BCOLS, BH, BW, D).transpose(0, 2, 1, 3, 4).reshape(lattice_lines * BH, BCOLS * BW, D)

    def to_blocks(field):
        placed = field.reshape(lattice_lines, BH, BCOLS, BW, D).transpose(0, 2, 1, 3, 4).reshape(BLOCKS, TOK, D)
        return jnp.roll(placed, -offset_blocks, axis=0).reshape(BLOCKS * TOK, D)

    def one_bin(state, inputs):
        frame, forgetting_speeds = inputs
        field = to_map(frame).astype(jnp.float32)
        padded = jnp.pad(field, ((1, 1), (0, 0), (0, 0)), mode='wrap')
        padded = jnp.pad(padded, ((0, 0), (1, 1), (0, 0)))
        height = lattice_lines * BH
        width = BCOLS * BW
        mixed = field
        for row_off in range(3):
            for col_off in range(3):
                mixed = mixed + mix_weight[3 * row_off + col_off] * padded[row_off:row_off + height, col_off:col_off + width]
        mixed = to_blocks(mixed)
        normed = rms_norm(mixed, gain_in)
        drive = jnp.dot(normed, in_weight, preferred_element_type=jnp.float32)
        state = forgetting_speeds[None] * state + jnp.sqrt(1.0 - forgetting_speeds * forgetting_speeds)[None] * drive
        state_b = state.astype(jnp.bfloat16)
        resid = mixed + jnp.dot(state_b, out_weight, preferred_element_type=jnp.float32) + skip_gain * normed.astype(jnp.float32)
        hidden = rms_norm(resid, feedforward_norm_gain)
        gate = jnp.dot(hidden, gate_weight, preferred_element_type=jnp.float32)
        upper = jnp.dot(hidden, up_weight, preferred_element_type=jnp.float32)
        gated = (jax.nn.silu(gate) * upper).astype(jnp.bfloat16)
        result = resid + jnp.dot(gated, down_weight, preferred_element_type=jnp.float32)
        return (state, result.astype(jnp.bfloat16).reshape(BLOCKS, TOK, D))
    start_state = jnp.zeros((BLOCKS * TOK, NS), jnp.float32)
    final_state, outputs = lax.scan(one_bin, start_state, (events, decay))
    return outputs
```

```python
import functools

import jax
import jax.numpy as jnp
from jax import lax
from jax.experimental import pallas as pl
from jax.experimental.pallas import tpu as pltpu
from jax.sharding import PartitionSpec as P

BH = 16
BW = 16
BCOLS = 4
EPS = 1e-05
INNER = tuple(range(4, 12))
OUTER = tuple(range(0, 4)) + tuple(range(12, 16))
HALF = len(INNER) * BW
FRONT_BINS = 4
BACK_BINS = 2


def neighbour_pairs(count, row_step, column_step):
    lines = count // BCOLS
    offset = BCOLS // 2
    pairs = []
    for source in range(count):
        place = (source + offset) % count
        row = (place // BCOLS + row_step) % lines
        column = place % BCOLS + column_step
        if 0 <= column < BCOLS:
            pairs.append((source, (row * BCOLS + column - offset) % count))
    return pairs


def front_kernel(rows, outer, *refs):
    if outer:
        (_, events, left, right, top, bottom, mix, gain, in_weight, skip, decay, inner_end,
         base, drive, end, edge, sides, normed, state) = refs
    else:
        (_, events, left, right, mix, gain, in_weight, skip, decay,
         base, drive, end, edge, sides, normed, state) = refs
    step = pl.program_id(0)
    bins = events.shape[0]
    width = events.shape[-1]

    @pl.when(step == 0)
    def _():
        state[...] = jnp.zeros_like(state)

    taps = [mix[k : k + 1, :] for k in range(9)]
    taps[4] = taps[4] + 1.0
    column = lax.broadcasted_iota(jnp.int32, (BW, width), 0)
    first, last = column == 0, column == BW - 1
    gain_row, skip_row = gain[...], skip[...]
    for b in range(bins):
        for side, ref in ((0, left), (1, right)):
            edge[side, 8:24, :] = ref[b].astype(jnp.float32)
            if outer:
                edge[side, 7:8, :] = top[b, BW + side : BW + side + 1, :].astype(jnp.float32)
                edge[side, 24:25, :] = bottom[b, BW + side : BW + side + 1, :].astype(jnp.float32)
            k = 2 * side
            sides[side, :, :] = (
                taps[k] * edge[side, 7:23, :]
                + taps[3 + k] * edge[side, 8:24, :]
                + taps[6 + k] * edge[side, 9:25, :]
            )
        cells = {}

        def row_of(i, b=b, cells=cells):
            if i not in cells:
                if i < 0:
                    value = top[b, 0:BW, :]
                elif i >= BH:
                    value = bottom[b, 0:BW, :]
                else:
                    value = events[b, 0, i * BW : (i + 1) * BW, :]
                cells[i] = value.astype(jnp.float32)
            return cells[i]

        for n, i in enumerate(rows):
            up, mid, down = row_of(i - 1), row_of(i), row_of(i + 1)
            from_left = taps[0] * up + taps[3] * mid + taps[6] * down
            centre = taps[1] * up + taps[4] * mid + taps[7] * down
            from_right = taps[2] * up + taps[5] * mid + taps[8] * down
            from_left = jnp.where(first, sides[0, i : i + 1, :], pltpu.roll(from_left, 1, 0))
            from_right = jnp.where(last, sides[1, i : i + 1, :], pltpu.roll(from_right, BW - 1, 0))
            mixed = centre + from_left + from_right
            power = jnp.mean(mixed * mixed, axis=-1, keepdims=True)
            scaled = (mixed * lax.rsqrt(power + EPS) * gain_row).astype(jnp.bfloat16)
            normed[b * HALF + n * BW : b * HALF + (n + 1) * BW, :] = scaled
            base[b, n * BW : (n + 1) * BW, :] = mixed + skip_row * scaled.astype(jnp.float32)
    product = jnp.dot(normed[...], in_weight[...], preferred_element_type=jnp.float32)
    for b in range(bins):
        rate = decay[pl.ds(step * bins + b, 1), :]
        term = product[b * HALF : (b + 1) * HALF] * jnp.sqrt(1.0 - rate * rate)
        drive[b, :, :] = term
        state[...] = rate * state[...] + term

    @pl.when(step == pl.num_programs(0) - 1)
    def _():
        if outer:
            end[0:HALF, :] = inner_end[...]
            end[HALF : 2 * HALF, :] = state[...].astype(jnp.bfloat16)
        else:
            end[...] = state[...].astype(jnp.bfloat16)


def fixed(shape):
    return pl.BlockSpec(shape, lambda i, where: (0,) * len(shape))


def by_bin(shape):
    return pl.BlockSpec(shape, lambda i, where: (i,) + (0,) * (len(shape) - 1))


def front(rows, outer, where, events, left, right, halos, mix, gain, in_weight, skip, decay, inner_end):
    count, width = events.shape[0], events.shape[-1]
    bins = FRONT_BINS
    operands = [events, left, right]
    specs = [by_bin((bins, 1, BH * BW, width)), by_bin((bins, BH, width)), by_bin((bins, BH, width))]
    for halo in halos:
        operands.append(halo)
        specs.append(by_bin((bins,) + halo.shape[1:]))
    operands += [mix, gain, in_weight, skip, decay]
    specs += [fixed(mix.shape), fixed(gain.shape), fixed(in_weight.shape), fixed(skip.shape)]
    specs.append(pl.BlockSpec((count, width), lambda i, where: (where[0], 0)))
    end_rows = HALF
    if outer:
        operands.append(inner_end)
        specs.append(fixed(inner_end.shape))
        end_rows = 2 * HALF
    return pl.pallas_call(
        functools.partial(front_kernel, rows, outer),
        grid_spec=pltpu.PrefetchScalarGridSpec(
            num_scalar_prefetch=1,
            grid=(count // bins,),
            in_specs=specs,
            out_specs=[
                by_bin((bins, HALF, width)),
                by_bin((bins, HALF, width)),
                fixed((end_rows, width)),
            ],
            scratch_shapes=[
                pltpu.VMEM((2, 32, width), jnp.float32),
                pltpu.VMEM((2, BH, width), jnp.float32),
                pltpu.VMEM((bins * HALF, width), jnp.bfloat16),
                pltpu.VMEM((HALF, width), jnp.float32),
            ],
        ),
        out_shape=[
            jax.ShapeDtypeStruct((count, HALF, width), jnp.float32),
            jax.ShapeDtypeStruct((count, HALF, width), jnp.float32),
            jax.ShapeDtypeStruct((end_rows, width), jnp.bfloat16),
        ],
        name="front_outer" if outer else "front_inner",
        compiler_params=pltpu.CompilerParams(vmem_limit_bytes=24 << 20),
        cost_estimate=pl.CostEstimate(
            flops=count * HALF * width * (2 * width + 40), bytes_accessed=7 << 20, transcendentals=0
        ),
    )(where, *operands)


def back_kernel(
    _, base_in, drive_in, base_out, drive_out, entering, decay, out_weight, gain, gate, upper, lower,
    result, state, held,
):
    step = pl.program_id(0)
    bins = base_in.shape[0]

    @pl.when(step == 0)
    def _():
        state[...] = entering[...].astype(jnp.float32)

    for b in range(bins):
        rate = decay[pl.ds(step * bins + b, 1), :]
        for part, drive in ((0, drive_in), (1, drive_out)):
            span = slice(part * HALF, (part + 1) * HALF)
            value = rate * state[span, :] + drive[b]
            state[span, :] = value
            held[b * 2 * HALF + part * HALF : b * 2 * HALF + (part + 1) * HALF, :] = value.astype(jnp.bfloat16)
    base = jnp.concatenate(
        [ref[b] for b in range(bins) for ref in (base_in, base_out)], axis=0
    )
    resid = base + jnp.dot(held[...], out_weight[...], preferred_element_type=jnp.float32)
    power = jnp.mean(resid * resid, axis=-1, keepdims=True)
    hidden = (resid * lax.rsqrt(power + EPS) * gain[...]).astype(jnp.bfloat16)
    width = resid.shape[-1]
    total = resid
    for n in range(gate.shape[-1] // width):
        part = slice(n * width, (n + 1) * width)
        opened = 0.5 * jnp.dot(hidden, gate[:, part], preferred_element_type=jnp.float32)
        raised = jnp.dot(hidden, upper[:, part], preferred_element_type=jnp.float32)
        gated = ((opened + opened * jnp.tanh(opened)) * raised).astype(jnp.bfloat16)
        total = total + jnp.dot(gated, lower[part, :], preferred_element_type=jnp.float32)
    done = total.astype(jnp.bfloat16)
    quarter = HALF // 2
    for b in range(bins):
        at = b * 2 * HALF
        result[b, 0, quarter : quarter + HALF, :] = done[at : at + HALF]
        result[b, 0, 0:quarter, :] = done[at + HALF : at + HALF + quarter]
        result[b, 0, quarter + HALF :, :] = done[at + HALF + quarter : at + 2 * HALF]


def back(where, base_in, drive_in, base_out, drive_out, entering, decay, out_weight, gain, gate, upper, lower):
    count, _, width = base_in.shape
    bins = BACK_BINS
    tokens = 2 * HALF
    block = by_bin((bins, HALF, width))
    return pl.pallas_call(
        back_kernel,
        grid_spec=pltpu.PrefetchScalarGridSpec(
            num_scalar_prefetch=1,
            grid=(count // bins,),
            in_specs=[
                block, block, block, block,
                fixed(entering.shape),
                pl.BlockSpec((count, width), lambda i, where: (where[0], 0)),
                fixed(out_weight.shape), fixed(gain.shape), fixed(gate.shape), fixed(upper.shape), fixed(lower.shape),
            ],
            out_specs=by_bin((bins, 1, tokens, width)),
            scratch_shapes=[
                pltpu.VMEM((tokens, width), jnp.float32),
                pltpu.VMEM((bins * tokens, width), jnp.bfloat16),
            ],
        ),
        out_shape=jax.ShapeDtypeStruct((count, 1, tokens, width), jnp.bfloat16),
        name="back",
        compiler_params=pltpu.CompilerParams(vmem_limit_bytes=32 << 20),
    )(where, base_in, drive_in, base_out, drive_out, entering, decay, out_weight, gain, gate, upper, lower)


def prefix_kernel(slots, decay, result):
    peers, _, width = slots.shape
    bins = decay.shape[0] // peers
    before = jnp.zeros(slots.shape[1:], jnp.float32)
    for k in range(peers):
        result[k] = before.astype(jnp.bfloat16)
        rate = decay[k * bins : (k + 1) * bins, :]
        rate = rate[0:8] * rate[8:16]
        for shift in (4, 2, 1):
            rate = rate * pltpu.roll(rate, shift, 0)
        before = rate[0:1] * before + slots[k].astype(jnp.float32)


def prefix(slots, decay):
    return pl.pallas_call(
        prefix_kernel,
        in_specs=[pl.BlockSpec(memory_space=pltpu.VMEM)] * 2,
        out_specs=pl.BlockSpec(memory_space=pltpu.VMEM),
        out_shape=jax.ShapeDtypeStruct(slots.shape, slots.dtype),
        name="prefix",
        compiler_params=pltpu.CompilerParams(vmem_limit_bytes=4 << 20),
    )(slots, decay)


def local(
    events, mix_weight, gain_in, in_weight, out_weight, skip_gain, feedforward_norm_gain,
    gate_weight, up_weight, down_weight, decay,
):
    bins_dev, _, tokens_dev, width = events.shape
    count = lax.axis_size("space")
    peers = lax.axis_size("tm")
    where = lax.axis_index("tm").astype(jnp.int32).reshape(1)
    frames = events.reshape(bins_dev, BH, BW, width)
    left = lax.ppermute(frames[:, :, BW - 1], "space", neighbour_pairs(count, 0, 1))
    right = lax.ppermute(frames[:, :, 0], "space", neighbour_pairs(count, 0, -1))

    def rim(row):
        return jnp.concatenate([frames[:, row], left[:, row : row + 1], right[:, row : row + 1]], axis=1)

    top = lax.ppermute(rim(BH - 1), "space", neighbour_pairs(count, 1, 0))
    bottom = lax.ppermute(rim(0), "space", neighbour_pairs(count, -1, 0))
    gain_row, skip_row = gain_in.reshape(1, width), skip_gain.reshape(1, width)
    shared = (mix_weight, gain_row, in_weight, skip_row, decay)
    base_in, drive_in, end_in = front(INNER, False, where, events, left, right, (), *shared, None)
    base_out, drive_out, ends = front(OUTER, True, where, events, left, right, (top, bottom), *shared, end_in)
    slots = lax.all_to_all(ends.reshape(peers, tokens_dev // peers, width), "tm", 0, 0)
    entering = lax.all_to_all(prefix(slots, decay), "tm", 0, 0).reshape(tokens_dev, width)
    return back(
        where, base_in, drive_in, base_out, drive_out, entering, decay, out_weight,
        feedforward_norm_gain.reshape(1, width), gate_weight, up_weight, down_weight,
    )


def solution(mesh):
    return jax.shard_map(
        local,
        mesh=mesh,
        in_specs=(P("tm", "space", None, None), P(), P(), P(), P(), P(), P(), P(), P(), P(), P()),
        out_specs=P("tm", "space", None, None),
        check_vma=False,
    )
```

```python
import functools

import jax
import jax.numpy as jnp
from jax import lax
from jax.experimental import pallas as pl
from jax.experimental.pallas import tpu as pltpu
from jax.sharding import PartitionSpec as P


BH = 16
BW = 16
BCOLS = 4
EPS = 1e-05
RIM = 24
INNER = tuple(range(2, 14))
OUTER = (0, 1, 14, 15)
FRONT_BINS = 4
BACK_BINS = 4
PACK_BINS = 2
STREAMS = 4


def neighbour_pairs(count, step_of):
    lines = count // BCOLS
    offset = BCOLS // 2
    pairs = []
    for source in range(count):
        place = (source + offset) % count
        row_step, column_step = step_of(place % BCOLS)
        row = (place // BCOLS + row_step) % lines
        column = place % BCOLS + column_step
        if 0 <= column < BCOLS:
            pairs.append((source, (row * BCOLS + column - offset) % count))
    return pairs


def in_hbm(array):
    return pltpu.with_memory_space_constraint(array, pltpu.HBM)


def pack_kernel(
    _, odd, *refs
):
    streams = refs[:STREAMS]
    mix, gain, skip, in_weight, decay, near, far, first_row, last_row, held, vectors, weight, rates = refs[STREAMS:]
    bins, _, tokens, _ = streams[0].shape
    share = held.shape[0] // STREAMS
    step = pl.program_id(0)

    @pl.when(step == 0)
    def _():
        vectors[0:9, :] = mix[...]
        vectors[9:10, :] = gain[...]
        vectors[10:11, :] = skip[...]
        weight[...] = in_weight[...]
        rates[...] = decay[...]

    row = lax.broadcasted_iota(jnp.int32, (2 * BH, tokens), 0)
    token = lax.broadcasted_iota(jnp.int32, (2 * BH, tokens), 1)
    facing = jnp.where(odd[0] == 1, 0, BW - 1)
    wanted = jnp.where(row < BH, row * BW + facing, (row - BH) * BW + (BW - 1 - facing))
    pick = (token == wanted).astype(jnp.float32).astype(jnp.bfloat16)
    for k, events in enumerate(streams):
        for b in range(bins):
            at = k * share + step * bins + b
            picked = jnp.dot(pick, events[b, 0], preferred_element_type=jnp.float32).astype(jnp.bfloat16)
            held[at, 0, :, :] = events[b, 0]
            near[at] = picked[0:BH]
            far[at] = picked[BH : 2 * BH]
            first_row[at] = events[b, 0, 0:BW, :]
            last_row[at] = events[b, 0, tokens - BW : tokens, :]


def pack(where, odd, events, mix, gain, skip, in_weight, decay):
    count, _, _, width = events.shape
    bins = PACK_BINS
    steps = count // (bins * STREAMS)
    edge = jax.ShapeDtypeStruct((count, BW, width), events.dtype)
    whole = pl.BlockSpec(memory_space=pltpu.VMEM)
    return pl.pallas_call(
        pack_kernel,
        grid_spec=pltpu.PrefetchScalarGridSpec(
            num_scalar_prefetch=2,
            grid=(steps,),
            in_specs=[
                pl.BlockSpec((bins,) + events.shape[1:], lambda i, where, _, k=k: (k * steps + i, 0, 0, 0))
                for k in range(STREAMS)
            ]
            + [
                fixed(mix.shape), fixed(gain.shape), fixed(skip.shape), fixed(in_weight.shape),
                pl.BlockSpec((count, width), lambda i, where, _: (where[0], 0)),
            ],
            out_specs=[whole] * 8,
        ),
        out_shape=[edge] * 4 + [
            jax.ShapeDtypeStruct(events.shape, events.dtype),
            jax.ShapeDtypeStruct((16, width), jnp.float32),
            jax.ShapeDtypeStruct(in_weight.shape, in_weight.dtype),
            jax.ShapeDtypeStruct((count, width), jnp.float32),
        ],
        name="pack",
        compiler_params=pltpu.CompilerParams(vmem_limit_bytes=16 << 20),
    )(where, odd, *(in_hbm(x) for x in (events,) * STREAMS + (mix, gain, skip, in_weight, decay)))


def rim_kernel(odd, near, far, first_row, last_row, down, up):
    place = lax.broadcasted_iota(jnp.int32, (RIM - BW, near.shape[-1]), 0)
    for b in range(near.shape[0]):
        left, right = sided(odd, near[b], far[b])
        for row, source, target in ((BH - 1, last_row, down), (0, first_row, up)):
            ends = jnp.where(place == 0, left[row : row + 1], jnp.where(place == 1, right[row : row + 1], 0.0))
            target[b, 0:BW, :] = source[b]
            target[b, BW:RIM, :] = ends.astype(jnp.bfloat16)


def sided(odd, near, far):
    near, far = near.astype(jnp.float32), far.astype(jnp.float32)
    flag = odd[0] == 1
    return jnp.where(flag, near, far), jnp.where(flag, far, near)


def rim(odd, near, far, first_row, last_row):
    count, _, width = near.shape
    whole = pl.BlockSpec(memory_space=pltpu.VMEM)
    return pl.pallas_call(
        rim_kernel,
        in_specs=[pl.BlockSpec(memory_space=pltpu.SMEM)] + [whole] * 4,
        out_specs=[whole] * 2,
        out_shape=[jax.ShapeDtypeStruct((count, RIM, width), near.dtype)] * 2,
        name="rim",
        compiler_params=pltpu.CompilerParams(vmem_limit_bytes=4 << 20),
    )(odd, near, far, first_row, last_row)


def front_kernel(rows, outer, *refs):
    if outer:
        (odd, events, near, far, top, bottom, vectors, in_weight, decay, inner_end,
         base, drive, end, edge, sides, normed, state) = refs
    else:
        (odd, events, near, far, vectors, in_weight, decay,
         base, drive, end, edge, sides, normed, state) = refs
    step = pl.program_id(0)
    bins = events.shape[0]
    width = events.shape[-1]
    size = len(rows) * BW

    @pl.when(step == 0)
    def _():
        state[...] = jnp.zeros_like(state)

    taps = [vectors[k : k + 1, :] for k in range(9)]
    taps[4] = taps[4] + 1.0
    column = lax.broadcasted_iota(jnp.int32, (BW, width), 0)
    first, last = column == 0, column == BW - 1
    gain_row, skip_row = vectors[9:10, :], vectors[10:11, :]
    for b in range(bins):
        for side, value in enumerate(sided(odd, near[b], far[b])):
            edge[side, 8:24, :] = value
            if outer:
                edge[side, 7:8, :] = top[b, BW + side : BW + side + 1, :].astype(jnp.float32)
                edge[side, 24:25, :] = bottom[b, BW + side : BW + side + 1, :].astype(jnp.float32)
            k = 2 * side
            sides[side, :, :] = (
                taps[k] * edge[side, 7:23, :]
                + taps[3 + k] * edge[side, 8:24, :]
                + taps[6 + k] * edge[side, 9:25, :]
            )
        cells = {}

        def row_of(i, b=b, cells=cells):
            if i not in cells:
                if i < 0:
                    value = top[b, 0:BW, :]
                elif i >= BH:
                    value = bottom[b, 0:BW, :]
                else:
                    value = events[b, 0, i * BW : (i + 1) * BW, :]
                cells[i] = value.astype(jnp.float32)
            return cells[i]

        for n, i in enumerate(rows):
            up, mid, down = row_of(i - 1), row_of(i), row_of(i + 1)
            from_left = taps[0] * up + taps[3] * mid + taps[6] * down
            centre = taps[1] * up + taps[4] * mid + taps[7] * down
            from_right = taps[2] * up + taps[5] * mid + taps[8] * down
            from_left = jnp.where(first, sides[0, i : i + 1, :], pltpu.roll(from_left, 1, 0))
            from_right = jnp.where(last, sides[1, i : i + 1, :], pltpu.roll(from_right, BW - 1, 0))
            mixed = centre + from_left + from_right
            power = jnp.mean(mixed * mixed, axis=-1, keepdims=True)
            scaled = (mixed * lax.rsqrt(power + EPS) * gain_row).astype(jnp.bfloat16)
            normed[b * size + n * BW : b * size + (n + 1) * BW, :] = scaled
            base[b, n * BW : (n + 1) * BW, :] = mixed + skip_row * scaled.astype(jnp.float32)
    product = jnp.dot(normed[...], in_weight[...], preferred_element_type=jnp.float32)
    for b in range(bins):
        rate = decay[pl.ds(step * bins + b, 1), :]
        term = product[b * size : (b + 1) * size] * jnp.sqrt(1.0 - rate * rate)
        drive[b, :, :] = term
        state[...] = rate * state[...] + term

    @pl.when(step == pl.num_programs(0) - 1)
    def _():
        if outer:
            end[0 : inner_end.shape[0], :] = inner_end[...]
            end[inner_end.shape[0] :, :] = state[...].astype(jnp.bfloat16)
        else:
            end[...] = state[...].astype(jnp.bfloat16)


def fixed(shape):
    return pl.BlockSpec(shape, lambda i, *_: (0,) * len(shape))


def by_bin(shape):
    return pl.BlockSpec(shape, lambda i, *_: (i,) + (0,) * (len(shape) - 1))


def front(rows, outer, odd, events, near, far, halos, vectors, in_weight, decay, inner_end):
    count, width = events.shape[0], events.shape[-1]
    bins = FRONT_BINS
    size = len(rows) * BW
    operands = [events, near, far]
    specs = [by_bin((bins, 1, BH * BW, width)), by_bin((bins, BH, width)), by_bin((bins, BH, width))]
    for halo in halos:
        operands.append(halo)
        specs.append(by_bin((bins,) + halo.shape[1:]))
    operands += [vectors, in_weight, decay]
    specs += [fixed(vectors.shape), fixed(in_weight.shape), fixed(decay.shape)]
    end_rows = size
    if outer:
        operands.append(inner_end)
        specs.append(fixed(inner_end.shape))
        end_rows = size + inner_end.shape[0]
    return pl.pallas_call(
        functools.partial(front_kernel, rows, outer),
        grid_spec=pltpu.PrefetchScalarGridSpec(
            num_scalar_prefetch=1,
            grid=(count // bins,),
            in_specs=specs,
            out_specs=[
                by_bin((bins, size, width)),
                by_bin((bins, size, width)),
                fixed((end_rows, width)),
            ],
            scratch_shapes=[
                pltpu.VMEM((2, 32, width), jnp.float32),
                pltpu.VMEM((2, BH, width), jnp.float32),
                pltpu.VMEM((bins * size, width), jnp.bfloat16),
                pltpu.VMEM((size, width), jnp.float32),
            ],
        ),
        out_shape=[
            jax.ShapeDtypeStruct((count, size, width), jnp.float32),
            jax.ShapeDtypeStruct((count, size, width), jnp.float32),
            jax.ShapeDtypeStruct((end_rows, width), jnp.bfloat16),
        ],
        name="front_outer" if outer else "front_inner",
        compiler_params=pltpu.CompilerParams(vmem_limit_bytes=24 << 20),
        cost_estimate=pl.CostEstimate(
            flops=count * size * width * (2 * width + 40), bytes_accessed=7 << 20, transcendentals=0
        ),
    )(odd, *operands)


def back_kernel(
    _, base_in, drive_in, base_out, drive_out, entering, decay, out_weight, gain, gate, upper, lower,
    result, state, held,
):
    step = pl.program_id(0)
    bins, inner, _ = base_in.shape
    tokens = result.shape[2]

    @pl.when(step == 0)
    def _():
        state[...] = entering[...].astype(jnp.float32)

    for b in range(bins):
        rate = decay[pl.ds(step * bins + b, 1), :]
        for start, drive in ((0, drive_in), (inner, drive_out)):
            stop = start + drive.shape[1]
            value = rate * state[start:stop, :] + drive[b]
            state[start:stop, :] = value
            held[b * tokens + start : b * tokens + stop, :] = value.astype(jnp.bfloat16)
    base = jnp.concatenate(
        [ref[b] for b in range(bins) for ref in (base_in, base_out)], axis=0
    )
    rows = base.shape[0]
    width = base.shape[-1]
    split = [slice(k * rows // 2, (k + 1) * rows // 2) for k in range(2)]

    def product(left, right):
        return jnp.concatenate(
            [jnp.dot(left[part], right, preferred_element_type=jnp.float32) for part in split], axis=0
        )

    resid = base + product(held[...], out_weight[...])
    power = jnp.mean(resid * resid, axis=-1, keepdims=True)
    hidden = (resid * lax.rsqrt(power + EPS) * gain[...]).astype(jnp.bfloat16)
    total = resid
    for n in range(gate.shape[-1] // width):
        part = slice(n * width, (n + 1) * width)
        opened = 0.5 * jnp.dot(hidden, gate[:, part], preferred_element_type=jnp.float32)
        raised = jnp.dot(hidden, upper[:, part], preferred_element_type=jnp.float32)
        gated = ((opened + opened * jnp.tanh(opened)) * raised).astype(jnp.bfloat16)
        total = total + product(gated, lower[part, :])
    done = total.astype(jnp.bfloat16)
    edge = (tokens - inner) // 2
    for b in range(bins):
        at = b * tokens
        result[b, 0, edge : edge + inner, :] = done[at : at + inner]
        result[b, 0, 0:edge, :] = done[at + inner : at + inner + edge]
        result[b, 0, edge + inner :, :] = done[at + inner + edge : at + tokens]


def back(where, base_in, drive_in, base_out, drive_out, entering, decay, out_weight, gain, gate, upper, lower):
    count, inner, width = base_in.shape
    outer = base_out.shape[1]
    bins = BACK_BINS
    tokens = inner + outer
    blocks = [by_bin((bins, size, width)) for size in (inner, inner, outer, outer)]
    return pl.pallas_call(
        back_kernel,
        grid_spec=pltpu.PrefetchScalarGridSpec(
            num_scalar_prefetch=1,
            grid=(count // bins,),
            in_specs=[
                *blocks,
                fixed(entering.shape),
                pl.BlockSpec((count, width), lambda i, where: (where[0], 0)),
                fixed(out_weight.shape), fixed(gain.shape), fixed(gate.shape), fixed(upper.shape), fixed(lower.shape),
            ],
            out_specs=by_bin((bins, 1, tokens, width)),
            scratch_shapes=[
                pltpu.VMEM((tokens, width), jnp.float32),
                pltpu.VMEM((bins * tokens, width), jnp.bfloat16),
            ],
        ),
        out_shape=jax.ShapeDtypeStruct((count, 1, tokens, width), jnp.bfloat16),
        name="back",
        compiler_params=pltpu.CompilerParams(vmem_limit_bytes=32 << 20),
    )(where, base_in, drive_in, base_out, drive_out, entering, decay, out_weight, gain, gate, upper, lower)


def prefix_kernel(slots, decay, result):
    peers, _, _ = slots.shape
    bins = decay.shape[0] // peers
    before = jnp.zeros(slots.shape[1:], jnp.float32)
    for k in range(peers):
        result[k] = before.astype(jnp.bfloat16)
        rate = decay[k * bins : (k + 1) * bins, :]
        rate = rate[0:8] * rate[8:16]
        for shift in (4, 2, 1):
            rate = rate * pltpu.roll(rate, shift, 0)
        before = rate[0:1] * before + slots[k].astype(jnp.float32)


def prefix(slots, decay):
    return pl.pallas_call(
        prefix_kernel,
        in_specs=[pl.BlockSpec(memory_space=pltpu.VMEM)] * 2,
        out_specs=pl.BlockSpec(memory_space=pltpu.VMEM),
        out_shape=jax.ShapeDtypeStruct(slots.shape, slots.dtype),
        name="prefix",
        compiler_params=pltpu.CompilerParams(vmem_limit_bytes=4 << 20),
    )(slots, decay)


def local(
    events, mix_weight, gain_in, in_weight, out_weight, skip_gain, feedforward_norm_gain,
    gate_weight, up_weight, down_weight, decay,
):
    _, _, tokens_dev, width = events.shape
    count = lax.axis_size("space")
    peers = lax.axis_size("tm")
    where = lax.axis_index("tm").astype(jnp.int32).reshape(1)
    odd = ((lax.axis_index("space") + BCOLS // 2) % 2).astype(jnp.int32).reshape(1)
    gain_row, skip_row = gain_in.reshape(1, width), skip_gain.reshape(1, width)
    near_edge, far_edge, first_row, last_row, held, *shared = pack(
        where, odd, events, mix_weight, gain_row, skip_row, in_weight, decay
    )
    far = lax.ppermute(far_edge, "space", neighbour_pairs(count, lambda c: (0, 1 if c % 2 else -1)))
    near = lax.ppermute(near_edge, "space", neighbour_pairs(count, lambda c: (0, -1 if c % 2 else 1)))
    down, up = rim(odd, near, far, first_row, last_row)
    top = lax.ppermute(down, "space", neighbour_pairs(count, lambda c: (1, 0)))
    bottom = lax.ppermute(up, "space", neighbour_pairs(count, lambda c: (-1, 0)))
    base_in, drive_in, end_in = front(INNER, False, odd, held, near, far, (), *shared, None)
    base_out, drive_out, ends = front(OUTER, True, odd, held, near, far, (top, bottom), *shared, end_in)
    slots = lax.all_to_all(ends.reshape(peers, tokens_dev // peers, width), "tm", 0, 0)
    entering = lax.all_to_all(prefix(slots, decay), "tm", 0, 0).reshape(tokens_dev, width)
    return back(
        where, base_in, drive_in, base_out, drive_out, entering, decay, out_weight,
        feedforward_norm_gain.reshape(1, width), gate_weight, up_weight, down_weight,
    )


def solution(mesh):
    return jax.shard_map(
        local,
        mesh=mesh,
        in_specs=(P("tm", "space", None, None), P(), P(), P(), P(), P(), P(), P(), P(), P(), P()),
        out_specs=P("tm", "space", None, None),
        check_vma=False,
    )
```

```python
import functools

import jax
import jax.numpy as jnp
from jax import lax
from jax.experimental import pallas as pl
from jax.experimental.pallas import tpu as pltpu
from jax.sharding import PartitionSpec as P


BH = 16
BW = 16
BCOLS = 4
EPS = 1e-05
RIM = 24
INNER = tuple(range(1, 15))
OUTER = (0, 15)
FRONT_BINS = 8
BACK_BINS = 4
PACK_BINS = 2
STREAMS = 4


def neighbour_pairs(count, step_of):
    lines = count // BCOLS
    offset = BCOLS // 2
    pairs = []
    for source in range(count):
        place = (source + offset) % count
        row_step, column_step = step_of(place % BCOLS)
        row = (place // BCOLS + row_step) % lines
        column = place % BCOLS + column_step
        if 0 <= column < BCOLS:
            pairs.append((source, (row * BCOLS + column - offset) % count))
    return pairs


def in_hbm(array):
    return pltpu.with_memory_space_constraint(array, pltpu.HBM)


def pack_kernel(
    _, odd, *refs
):
    streams = refs[:STREAMS]
    mix, gain, in_weight, decay, near, far, first_row, last_row, held, vectors, weight, rates = refs[STREAMS:]
    bins, _, tokens, width = streams[0].shape
    share = held.shape[0] // STREAMS
    step = pl.program_id(0)

    @pl.when(step == 0)
    def _():
        vectors[0:9, :] = mix[...]
        vectors[9:10, :] = gain[...]
        weight[...] = in_weight[...]
        rate = decay[...]
        count = rate.shape[0]
        scale = jnp.sqrt(1.0 - rate * rate)
        rates[0:count, :] = rate
        rates[count : 2 * count, :] = scale
        tail = jnp.ones((1, width), jnp.float32)
        for t in reversed(range(count)):
            rates[2 * count + t : 2 * count + t + 1, :] = scale[t : t + 1] * tail
            tail = tail * rate[t : t + 1]

    row = lax.broadcasted_iota(jnp.int32, (2 * BH, tokens), 0)
    token = lax.broadcasted_iota(jnp.int32, (2 * BH, tokens), 1)
    facing = jnp.where(odd[0] == 1, 0, BW - 1)
    wanted = jnp.where(row < BH, row * BW + facing, (row - BH) * BW + (BW - 1 - facing))
    pick = (token == wanted).astype(jnp.float32).astype(jnp.bfloat16)
    for k, events in enumerate(streams):
        for b in range(bins):
            at = k * share + step * bins + b
            picked = jnp.dot(pick, events[b, 0], preferred_element_type=jnp.float32).astype(jnp.bfloat16)
            held[at, 0, :, :] = events[b, 0]
            near[at] = picked[0:BH]
            far[at] = picked[BH : 2 * BH]
            first_row[at] = events[b, 0, 0:BW, :]
            last_row[at] = events[b, 0, tokens - BW : tokens, :]


def pack(where, odd, events, mix, gain, in_weight, decay):
    count, _, _, width = events.shape
    bins = PACK_BINS
    steps = count // (bins * STREAMS)
    edge = jax.ShapeDtypeStruct((count, BW, width), events.dtype)
    whole = pl.BlockSpec(memory_space=pltpu.VMEM)
    return pl.pallas_call(
        pack_kernel,
        grid_spec=pltpu.PrefetchScalarGridSpec(
            num_scalar_prefetch=2,
            grid=(steps,),
            in_specs=[
                pl.BlockSpec((bins,) + events.shape[1:], lambda i, where, _, k=k: (k * steps + i, 0, 0, 0))
                for k in range(STREAMS)
            ]
            + [
                fixed(mix.shape), fixed(gain.shape), fixed(in_weight.shape),
                pl.BlockSpec((count, width), lambda i, where, _: (where[0], 0)),
            ],
            out_specs=[whole] * 8,
        ),
        out_shape=[edge] * 4 + [
            jax.ShapeDtypeStruct(events.shape, events.dtype),
            jax.ShapeDtypeStruct((16, width), jnp.float32),
            jax.ShapeDtypeStruct(in_weight.shape, in_weight.dtype),
            jax.ShapeDtypeStruct((3 * count, width), jnp.float32),
        ],
        name="pack",
        compiler_params=pltpu.CompilerParams(vmem_limit_bytes=16 << 20),
    )(where, odd, *(in_hbm(x) for x in (events,) * STREAMS + (mix, gain, in_weight, decay)))


def rim_kernel(odd, near, far, first_row, last_row, down, up):
    place = lax.broadcasted_iota(jnp.int32, (RIM - BW, near.shape[-1]), 0)
    for b in range(near.shape[0]):
        left, right = sided(odd, near[b], far[b])
        for row, source, target in ((BH - 1, last_row, down), (0, first_row, up)):
            ends = jnp.where(place == 0, left[row : row + 1], jnp.where(place == 1, right[row : row + 1], 0.0))
            target[b, 0:BW, :] = source[b]
            target[b, BW:RIM, :] = ends.astype(jnp.bfloat16)


def sided(odd, near, far):
    near, far = near.astype(jnp.float32), far.astype(jnp.float32)
    flag = odd[0] == 1
    return jnp.where(flag, near, far), jnp.where(flag, far, near)


def rim(odd, near, far, first_row, last_row):
    count, _, width = near.shape
    whole = pl.BlockSpec(memory_space=pltpu.VMEM)
    return pl.pallas_call(
        rim_kernel,
        in_specs=[pl.BlockSpec(memory_space=pltpu.SMEM)] + [whole] * 4,
        out_specs=[whole] * 2,
        out_shape=[jax.ShapeDtypeStruct((count, RIM, width), near.dtype)] * 2,
        name="rim",
        compiler_params=pltpu.CompilerParams(vmem_limit_bytes=4 << 20),
    )(odd, near, far, first_row, last_row)


def front_kernel(rows, outer, *refs):
    if outer:
        (odd, events, near, far, top, bottom, vectors, in_weight, rates, inner_end,
         mixture, normed, drive, end, edge, sides, state) = refs
    else:
        (odd, events, near, far, vectors, in_weight, rates,
         mixture, normed, drive, end, edge, sides, state) = refs
    step = pl.program_id(0)
    bins = events.shape[0] if outer else FRONT_BINS
    width = events.shape[-1]
    size = len(rows) * BW

    @pl.when(step == 0)
    def _():
        state[...] = jnp.zeros_like(state)

    taps = [vectors[k : k + 1, :] for k in range(9)]
    taps[4] = taps[4] + 1.0
    column = lax.broadcasted_iota(jnp.int32, (BW // 2, width), 0)
    first, last = column == 0, column == BW // 2 - 1
    gain_row = vectors[9:10, :]
    count = events.shape[0]
    for b in range(bins):
        at = step * bins + b
        for side, value in enumerate(sided(odd, near[at], far[at])):
            edge[side, 8:24, :] = value
            if outer:
                edge[side, 7:8, :] = top[at, BW + side : BW + side + 1, :].astype(jnp.float32)
                edge[side, 24:25, :] = bottom[at, BW + side : BW + side + 1, :].astype(jnp.float32)
            k = 2 * side
            sides[side, :, :] = (
                taps[k] * edge[side, 7:23, :]
                + taps[3 + k] * edge[side, 8:24, :]
                + taps[6 + k] * edge[side, 9:25, :]
            )
        cells = {}

        def row_of(i, at=at, cells=cells):
            if i not in cells:
                if i < 0:
                    value = top[at, 0:BW, :]
                elif i >= BH:
                    value = bottom[at, 0:BW, :]
                else:
                    value = events[at, 0, i * BW : (i + 1) * BW, :]
                cells[i] = value.astype(jnp.float32)
            return cells[i]

        for n, i in enumerate(rows):
            up, mid, down = row_of(i - 1), row_of(i), row_of(i + 1)
            from_left = taps[0] * up + taps[3] * mid + taps[6] * down
            centre = taps[1] * up + taps[4] * mid + taps[7] * down
            from_right = taps[2] * up + taps[5] * mid + taps[8] * down
            low = pltpu.roll(from_left[: BW // 2], 1, 0)
            high = pltpu.roll(from_left[BW // 2 :], 1, 0)
            from_left = jnp.concatenate(
                [jnp.where(first, sides[0, i : i + 1, :], low), jnp.where(first, low, high)], axis=0
            )
            low = pltpu.roll(from_right[: BW // 2], BW // 2 - 1, 0)
            high = pltpu.roll(from_right[BW // 2 :], BW // 2 - 1, 0)
            from_right = jnp.concatenate(
                [jnp.where(last, high, low), jnp.where(last, sides[1, i : i + 1, :], high)], axis=0
            )
            mixed = centre + from_left + from_right
            power = jnp.mean(mixed * mixed, axis=-1, keepdims=True)
            mixture[at, n * BW : (n + 1) * BW, :] = mixed
            normed[at, n * BW : (n + 1) * BW, :] = (mixed * lax.rsqrt(power + EPS) * gain_row).astype(jnp.bfloat16)
    rows_now = normed[pl.ds(step * bins, bins)].reshape(bins * size, width)
    product = jnp.dot(rows_now, in_weight[...], preferred_element_type=jnp.float32)
    total = state[...]
    for b in range(bins):
        term = product[b * size : (b + 1) * size]
        drive[step * bins + b, :, :] = term
        total = total + rates[pl.ds(2 * count + step * bins + b, 1), :] * term
    state[...] = total

    @pl.when(step == pl.num_programs(0) - 1)
    def _():
        if outer:
            end[0 : inner_end.shape[0], :] = inner_end[...]
            end[inner_end.shape[0] :, :] = state[...].astype(jnp.bfloat16)
        else:
            end[...] = state[...].astype(jnp.bfloat16)


def fixed(shape):
    return pl.BlockSpec(shape, lambda i, *_: (0,) * len(shape))


def by_bin(shape):
    return pl.BlockSpec(shape, lambda i, *_: (i,) + (0,) * (len(shape) - 1))


def front(rows, outer, odd, events, near, far, halos, vectors, in_weight, decay, inner_end):
    count, width = events.shape[0], events.shape[-1]
    bins = count if outer else FRONT_BINS
    size = len(rows) * BW
    whole = pl.BlockSpec(memory_space=pltpu.VMEM)
    operands = [events, near, far, *halos, vectors, in_weight, decay]
    end_rows = size
    if outer:
        operands.append(inner_end)
        end_rows = size + inner_end.shape[0]
    return pl.pallas_call(
        functools.partial(front_kernel, rows, outer),
        grid_spec=pltpu.PrefetchScalarGridSpec(
            num_scalar_prefetch=1,
            grid=(count // bins,),
            in_specs=[whole] * len(operands),
            out_specs=[whole] * 4,
            scratch_shapes=[
                pltpu.VMEM((2, 32, width), jnp.float32),
                pltpu.VMEM((2, BH, width), jnp.float32),
                pltpu.VMEM((size, width), jnp.float32),
            ],
        ),
        out_shape=[
            jax.ShapeDtypeStruct((count, size, width), jnp.float32),
            jax.ShapeDtypeStruct((count, size, width), jnp.bfloat16),
            jax.ShapeDtypeStruct((count, size, width), jnp.float32),
            jax.ShapeDtypeStruct((end_rows, width), jnp.bfloat16),
        ],
        name="front_outer" if outer else "front_inner",
        compiler_params=pltpu.CompilerParams(vmem_limit_bytes=24 << 20),
        cost_estimate=pl.CostEstimate(
            flops=count * size * width * (2 * width + 40), bytes_accessed=7 << 20, transcendentals=0
        ),
    )(odd, *operands)


def back_kernel(
    mixed_in, normed_in, drive_in, mixed_out, normed_out, drive_out, entering, rates, out_weight, skip, gain,
    gate, upper, lower, result, state, held,
):
    step = pl.program_id(0)
    bins, inner = BACK_BINS, mixed_in.shape[1]
    count = mixed_in.shape[0]
    tokens = result.shape[2]

    @pl.when(step == 0)
    def _():
        state[...] = entering[...].astype(jnp.float32)

    for b in range(bins):
        rate = rates[pl.ds(step * bins + b, 1), :]
        scale = rates[pl.ds(count + step * bins + b, 1), :]
        for start, drive in ((0, drive_in), (inner, drive_out)):
            stop = start + drive.shape[1]
            value = rate * state[start:stop, :] + scale * drive[step * bins + b]
            state[start:stop, :] = value
            held[b * tokens + start : b * tokens + stop, :] = value.astype(jnp.bfloat16)
    skip_row = skip[...]
    base = jnp.concatenate(
        [
            mixed[step * bins + b] + skip_row * normed[step * bins + b].astype(jnp.float32)
            for b in range(bins)
            for mixed, normed in ((mixed_in, normed_in), (mixed_out, normed_out))
        ],
        axis=0,
    )
    rows = base.shape[0]
    width = base.shape[-1]
    split = [slice(k * rows // 2, (k + 1) * rows // 2) for k in range(2)]

    def product(left, right):
        return jnp.concatenate(
            [jnp.dot(left[part], right, preferred_element_type=jnp.float32) for part in split], axis=0
        )

    resid = base + product(held[...], out_weight[...])
    power = jnp.mean(resid * resid, axis=-1, keepdims=True)
    hidden = (resid * lax.rsqrt(power + EPS) * gain[...]).astype(jnp.bfloat16)
    total = resid
    for n in range(gate.shape[-1] // width):
        part = slice(n * width, (n + 1) * width)
        opened = 0.5 * jnp.dot(hidden, gate[:, part], preferred_element_type=jnp.float32)
        raised = jnp.dot(hidden, upper[:, part], preferred_element_type=jnp.float32)
        gated = ((opened + opened * jnp.tanh(opened)) * raised).astype(jnp.bfloat16)
        total = total + product(gated, lower[part, :])
    done = total.astype(jnp.bfloat16)
    edge = (tokens - inner) // 2
    for b in range(bins):
        at = b * tokens
        result[b, 0, edge : edge + inner, :] = done[at : at + inner]
        result[b, 0, 0:edge, :] = done[at + inner : at + inner + edge]
        result[b, 0, edge + inner :, :] = done[at + inner + edge : at + tokens]


def back(inner_parts, outer_parts, *others):
    count, inner, width = inner_parts[0].shape
    outer = outer_parts[0].shape[1]
    bins = BACK_BINS
    tokens = inner + outer
    whole = pl.BlockSpec(memory_space=pltpu.VMEM)
    return pl.pallas_call(
        back_kernel,
        grid_spec=pltpu.PrefetchScalarGridSpec(
            num_scalar_prefetch=0,
            grid=(count // bins,),
            in_specs=[whole] * (6 + len(others)),
            out_specs=by_bin((bins, 1, tokens, width)),
            scratch_shapes=[
                pltpu.VMEM((tokens, width), jnp.float32),
                pltpu.VMEM((bins * tokens, width), jnp.bfloat16),
            ],
        ),
        out_shape=jax.ShapeDtypeStruct((count, 1, tokens, width), jnp.bfloat16),
        name="back",
        compiler_params=pltpu.CompilerParams(vmem_limit_bytes=32 << 20),
    )(*inner_parts, *outer_parts, *others)


def prefix_kernel(slots, decay, result):
    peers, _, _ = slots.shape
    bins = decay.shape[0] // peers
    before = jnp.zeros(slots.shape[1:], jnp.float32)
    for k in range(peers):
        result[k] = before.astype(jnp.bfloat16)
        rate = decay[k * bins : (k + 1) * bins, :]
        rate = rate[0:8] * rate[8:16]
        for shift in (4, 2, 1):
            rate = rate * pltpu.roll(rate, shift, 0)
        before = rate[0:1] * before + slots[k].astype(jnp.float32)


def prefix(slots, decay):
    return pl.pallas_call(
        prefix_kernel,
        in_specs=[pl.BlockSpec(memory_space=pltpu.VMEM)] * 2,
        out_specs=pl.BlockSpec(memory_space=pltpu.VMEM),
        out_shape=jax.ShapeDtypeStruct(slots.shape, slots.dtype),
        name="prefix",
        compiler_params=pltpu.CompilerParams(vmem_limit_bytes=4 << 20),
    )(slots, decay)


def local(
    events, mix_weight, gain_in, in_weight, out_weight, skip_gain, feedforward_norm_gain,
    gate_weight, up_weight, down_weight, decay,
):
    _, _, tokens_dev, width = events.shape
    count = lax.axis_size("space")
    peers = lax.axis_size("tm")
    where = lax.axis_index("tm").astype(jnp.int32).reshape(1)
    odd = ((lax.axis_index("space") + BCOLS // 2) % 2).astype(jnp.int32).reshape(1)
    gain_row, skip_row = gain_in.reshape(1, width), skip_gain.reshape(1, width)
    near_edge, far_edge, first_row, last_row, held, *shared = pack(
        where, odd, events, mix_weight, gain_row, in_weight, decay
    )
    far = lax.ppermute(far_edge, "space", neighbour_pairs(count, lambda c: (0, 1 if c % 2 else -1)))
    near = lax.ppermute(near_edge, "space", neighbour_pairs(count, lambda c: (0, -1 if c % 2 else 1)))
    down, up = rim(odd, near, far, first_row, last_row)
    top = lax.ppermute(down, "space", neighbour_pairs(count, lambda c: (1, 0)))
    bottom = lax.ppermute(up, "space", neighbour_pairs(count, lambda c: (-1, 0)))
    *inner_parts, end_in = front(INNER, False, odd, held, near, far, (), *shared, None)
    *outer_parts, ends = front(OUTER, True, odd, held, near, far, (top, bottom), *shared, end_in)
    slots = lax.all_to_all(ends.reshape(peers, tokens_dev // peers, width), "tm", 0, 0)
    entering = lax.all_to_all(prefix(slots, decay), "tm", 0, 0).reshape(tokens_dev, width)
    return back(
        inner_parts, outer_parts, entering, shared[2], out_weight, skip_row,
        feedforward_norm_gain.reshape(1, width), gate_weight, up_weight, down_weight,
    )


def solution(mesh):
    return jax.shard_map(
        local,
        mesh=mesh,
        in_specs=(P("tm", "space", None, None), P(), P(), P(), P(), P(), P(), P(), P(), P(), P()),
        out_specs=P("tm", "space", None, None),
        check_vma=False,
    )
```

```python
import functools

import jax
import jax.numpy as jnp
from jax import lax
from jax.experimental import pallas as pl
from jax.experimental.pallas import tpu as pltpu
from jax.sharding import PartitionSpec as P


BH = 16
BW = 16
BCOLS = 4
EPS = 1e-05
RIM = 24
INNER = tuple(range(1, 15))
OUTER = (0, 15)
FRONT_BINS = 8
BACK_BINS = 4
PACK_BINS = 2
STREAMS = 4


def neighbour_pairs(count, step_of):
    lines = count // BCOLS
    offset = BCOLS // 2
    pairs = []
    for source in range(count):
        place = (source + offset) % count
        row_step, column_step = step_of(place % BCOLS)
        row = (place // BCOLS + row_step) % lines
        column = place % BCOLS + column_step
        if 0 <= column < BCOLS:
            pairs.append((source, (row * BCOLS + column - offset) % count))
    return pairs


def in_hbm(array):
    return pltpu.with_memory_space_constraint(array, pltpu.HBM)


def pack_kernel(
    _, odd, *refs
):
    streams = refs[:STREAMS]
    mix, gain, in_weight, decay, near, far, first_row, last_row, held, vectors, weight, rates = refs[STREAMS:]
    bins, _, tokens, width = streams[0].shape
    share = held.shape[0] // STREAMS
    step = pl.program_id(0)

    @pl.when(step == 0)
    def _():
        vectors[0:9, :] = mix[...]
        vectors[9:10, :] = gain[...]
        weight[...] = in_weight[...]
        rate = decay[...]
        count = rate.shape[0]
        scale = jnp.sqrt(1.0 - rate * rate)
        rates[0:count, :] = rate
        rates[count : 2 * count, :] = scale
        tail = jnp.ones((1, width), jnp.float32)
        for t in reversed(range(count)):
            rates[2 * count + t : 2 * count + t + 1, :] = scale[t : t + 1] * tail
            tail = tail * rate[t : t + 1]

    row = lax.broadcasted_iota(jnp.int32, (2 * BH, tokens), 0)
    token = lax.broadcasted_iota(jnp.int32, (2 * BH, tokens), 1)
    facing = jnp.where(odd[0] == 1, 0, BW - 1)
    wanted = jnp.where(row < BH, row * BW + facing, (row - BH) * BW + (BW - 1 - facing))
    pick = (token == wanted).astype(jnp.float32).astype(jnp.bfloat16)
    for k, events in enumerate(streams):
        for b in range(bins):
            at = k * share + step * bins + b
            picked = jnp.dot(pick, events[b, 0], preferred_element_type=jnp.float32).astype(jnp.bfloat16)
            held[at, 0, :, :] = events[b, 0]
            near[at] = picked[0:BH]
            far[at] = picked[BH : 2 * BH]
            first_row[at] = events[b, 0, 0:BW, :]
            last_row[at] = events[b, 0, tokens - BW : tokens, :]


def pack(where, odd, events, mix, gain, in_weight, decay):
    count, _, _, width = events.shape
    bins = PACK_BINS
    steps = count // (bins * STREAMS)
    edge = jax.ShapeDtypeStruct((count, BW, width), events.dtype)
    whole = pl.BlockSpec(memory_space=pltpu.VMEM)
    return pl.pallas_call(
        pack_kernel,
        grid_spec=pltpu.PrefetchScalarGridSpec(
            num_scalar_prefetch=2,
            grid=(steps,),
            in_specs=[
                pl.BlockSpec((bins,) + events.shape[1:], lambda i, where, _, k=k: (k * steps + i, 0, 0, 0))
                for k in range(STREAMS)
            ]
            + [
                fixed(mix.shape), fixed(gain.shape), fixed(in_weight.shape),
                pl.BlockSpec((count, width), lambda i, where, _: (where[0], 0)),
            ],
            out_specs=[whole] * 8,
        ),
        out_shape=[edge] * 4 + [
            jax.ShapeDtypeStruct(events.shape, events.dtype),
            jax.ShapeDtypeStruct((16, width), jnp.float32),
            jax.ShapeDtypeStruct(in_weight.shape, in_weight.dtype),
            jax.ShapeDtypeStruct((3 * count, width), jnp.float32),
        ],
        name="pack",
        compiler_params=pltpu.CompilerParams(vmem_limit_bytes=16 << 20),
    )(where, odd, *(in_hbm(x) for x in (events,) * STREAMS + (mix, gain, in_weight, decay)))


def rim_kernel(odd, near, far, first_row, last_row, down, up):
    place = lax.broadcasted_iota(jnp.int32, (RIM - BW, near.shape[-1]), 0)
    for b in range(near.shape[0]):
        left, right = sided(odd, near[b], far[b])
        for row, source, target in ((BH - 1, last_row, down), (0, first_row, up)):
            ends = jnp.where(place == 0, left[row : row + 1], jnp.where(place == 1, right[row : row + 1], 0.0))
            target[b, 0:BW, :] = source[b]
            target[b, BW:RIM, :] = ends.astype(jnp.bfloat16)


def sided(odd, near, far):
    near, far = near.astype(jnp.float32), far.astype(jnp.float32)
    flag = odd[0] == 1
    return jnp.where(flag, near, far), jnp.where(flag, far, near)


def rim(odd, near, far, first_row, last_row):
    count, _, width = near.shape
    whole = pl.BlockSpec(memory_space=pltpu.VMEM)
    return pl.pallas_call(
        rim_kernel,
        in_specs=[pl.BlockSpec(memory_space=pltpu.SMEM)] + [whole] * 4,
        out_specs=[whole] * 2,
        out_shape=[jax.ShapeDtypeStruct((count, RIM, width), near.dtype)] * 2,
        name="rim",
        compiler_params=pltpu.CompilerParams(vmem_limit_bytes=4 << 20),
    )(odd, near, far, first_row, last_row)


def front_kernel(rows, outer, *refs):
    if outer:
        (odd, events, near, far, top, bottom, vectors, in_weight, rates, inner_end,
         mixture, normed, drive, end, edge, sides, state) = refs
    else:
        (odd, events, near, far, vectors, in_weight, rates,
         mixture, normed, drive, end, edge, sides, state) = refs
    step = pl.program_id(0)
    bins = events.shape[0] if outer else FRONT_BINS
    width = events.shape[-1]
    size = len(rows) * BW

    @pl.when(step == 0)
    def _():
        state[...] = jnp.zeros_like(state)

    taps = [vectors[k : k + 1, :] for k in range(9)]
    taps[4] = taps[4] + 1.0
    column = lax.broadcasted_iota(jnp.int32, (BW // 2, width), 0)
    first, last = column == 0, column == BW // 2 - 1
    gain_row = vectors[9:10, :]
    count = events.shape[0]
    for b in range(bins):
        at = step * bins + b
        for side, value in enumerate(sided(odd, near[at], far[at])):
            edge[side, 8:24, :] = value
            if outer:
                edge[side, 7:8, :] = top[at, BW + side : BW + side + 1, :].astype(jnp.float32)
                edge[side, 24:25, :] = bottom[at, BW + side : BW + side + 1, :].astype(jnp.float32)
            k = 2 * side
            sides[side, :, :] = (
                taps[k] * edge[side, 7:23, :]
                + taps[3 + k] * edge[side, 8:24, :]
                + taps[6 + k] * edge[side, 9:25, :]
            )
        cells = {}

        def row_of(i, at=at, cells=cells):
            if i not in cells:
                if i < 0:
                    value = top[at, 0:BW, :]
                elif i >= BH:
                    value = bottom[at, 0:BW, :]
                else:
                    value = events[at, 0, i * BW : (i + 1) * BW, :]
                cells[i] = value.astype(jnp.float32)
            return cells[i]

        for n, i in enumerate(rows):
            up, mid, down = row_of(i - 1), row_of(i), row_of(i + 1)
            from_left = taps[0] * up + taps[3] * mid + taps[6] * down
            centre = taps[1] * up + taps[4] * mid + taps[7] * down
            from_right = taps[2] * up + taps[5] * mid + taps[8] * down
            low = pltpu.roll(from_left[: BW // 2], 1, 0)
            high = pltpu.roll(from_left[BW // 2 :], 1, 0)
            from_left = jnp.concatenate(
                [jnp.where(first, sides[0, i : i + 1, :], low), jnp.where(first, low, high)], axis=0
            )
            low = pltpu.roll(from_right[: BW // 2], BW // 2 - 1, 0)
            high = pltpu.roll(from_right[BW // 2 :], BW // 2 - 1, 0)
            from_right = jnp.concatenate(
                [jnp.where(last, high, low), jnp.where(last, sides[1, i : i + 1, :], high)], axis=0
            )
            mixed = centre + from_left + from_right
            power = jnp.mean(mixed * mixed, axis=-1, keepdims=True)
            mixture[at, n * BW : (n + 1) * BW, :] = mixed
            normed[at, n * BW : (n + 1) * BW, :] = (mixed * lax.rsqrt(power + EPS) * gain_row).astype(jnp.bfloat16)
    rows_now = normed[pl.ds(step * bins, bins)].reshape(bins * size, width)
    product = jnp.dot(rows_now, in_weight[...], preferred_element_type=jnp.float32)
    total = state[...]
    for b in range(bins):
        term = product[b * size : (b + 1) * size]
        drive[step * bins + b, :, :] = term
        total = total + rates[pl.ds(2 * count + step * bins + b, 1), :] * term
    state[...] = total

    @pl.when(step == pl.num_programs(0) - 1)
    def _():
        if outer:
            end[0 : inner_end.shape[0], :] = inner_end[...]
            end[inner_end.shape[0] :, :] = state[...].astype(jnp.bfloat16)
        else:
            end[...] = state[...].astype(jnp.bfloat16)


def fixed(shape):
    return pl.BlockSpec(shape, lambda i, *_: (0,) * len(shape))


def by_bin(shape):
    return pl.BlockSpec(shape, lambda i, *_: (i,) + (0,) * (len(shape) - 1))


def front(rows, outer, odd, events, near, far, halos, vectors, in_weight, decay, inner_end):
    count, width = events.shape[0], events.shape[-1]
    bins = count if outer else FRONT_BINS
    size = len(rows) * BW
    whole = pl.BlockSpec(memory_space=pltpu.VMEM)
    operands = [events, near, far, *halos, vectors, in_weight, decay]
    end_rows = size
    if outer:
        operands.append(inner_end)
        end_rows = size + inner_end.shape[0]
    return pl.pallas_call(
        functools.partial(front_kernel, rows, outer),
        grid_spec=pltpu.PrefetchScalarGridSpec(
            num_scalar_prefetch=1,
            grid=(count // bins,),
            in_specs=[whole] * len(operands),
            out_specs=[whole] * 4,
            scratch_shapes=[
                pltpu.VMEM((2, 32, width), jnp.float32),
                pltpu.VMEM((2, BH, width), jnp.float32),
                pltpu.VMEM((size, width), jnp.float32),
            ],
        ),
        out_shape=[
            jax.ShapeDtypeStruct((count, size, width), jnp.float32),
            jax.ShapeDtypeStruct((count, size, width), jnp.bfloat16),
            jax.ShapeDtypeStruct((count, size, width), jnp.float32),
            jax.ShapeDtypeStruct((end_rows, width), jnp.bfloat16),
        ],
        name="front_outer" if outer else "front_inner",
        compiler_params=pltpu.CompilerParams(vmem_limit_bytes=24 << 20),
        cost_estimate=pl.CostEstimate(
            flops=count * size * width * (2 * width + 40), bytes_accessed=7 << 20, transcendentals=0
        ),
    )(odd, *operands)


def back_kernel(
    mixed_in, normed_in, drive_in, mixed_out, normed_out, drive_out, entering, rates, out_weight, skip, gain,
    gate, upper, lower, result, state, held, halved,
):
    step = pl.program_id(0)
    bins, inner = BACK_BINS, mixed_in.shape[1]
    count = mixed_in.shape[0]
    tokens = result.shape[2]

    @pl.when(step == 0)
    def _():
        state[...] = entering[...].astype(jnp.float32)
        halved[...] = (gate[...].astype(jnp.float32) * 0.5).astype(jnp.bfloat16)

    for b in range(bins):
        rate = rates[pl.ds(step * bins + b, 1), :]
        scale = rates[pl.ds(count + step * bins + b, 1), :]
        for start, drive in ((0, drive_in), (inner, drive_out)):
            stop = start + drive.shape[1]
            value = rate * state[start:stop, :] + scale * drive[step * bins + b]
            state[start:stop, :] = value
            held[b * tokens + start : b * tokens + stop, :] = value.astype(jnp.bfloat16)
    skip_row = skip[...]
    base = jnp.concatenate(
        [
            mixed[step * bins + b] + skip_row * normed[step * bins + b].astype(jnp.float32)
            for b in range(bins)
            for mixed, normed in ((mixed_in, normed_in), (mixed_out, normed_out))
        ],
        axis=0,
    )
    rows = base.shape[0]
    width = base.shape[-1]
    split = [slice(k * rows // 4, (k + 1) * rows // 4) for k in range(4)]

    def product(left, right):
        return jnp.concatenate(
            [jnp.dot(left[part], right, preferred_element_type=jnp.float32) for part in split], axis=0
        )

    resid = base + product(held[...], out_weight[...])
    power = jnp.mean(resid * resid, axis=-1, keepdims=True)
    hidden = (resid * lax.rsqrt(power + EPS) * gain[...]).astype(jnp.bfloat16)
    total = resid
    for n in range(gate.shape[-1] // width):
        part = slice(n * width, (n + 1) * width)
        opened = jnp.dot(hidden, halved[:, part], preferred_element_type=jnp.float32)
        raised = jnp.dot(hidden, upper[:, part], preferred_element_type=jnp.float32)
        gated = ((opened + opened * jnp.tanh(opened)) * raised).astype(jnp.bfloat16)
        total = total + product(gated, lower[part, :])
    done = total.astype(jnp.bfloat16)
    edge = (tokens - inner) // 2
    for b in range(bins):
        at = b * tokens
        result[b, 0, edge : edge + inner, :] = done[at : at + inner]
        result[b, 0, 0:edge, :] = done[at + inner : at + inner + edge]
        result[b, 0, edge + inner :, :] = done[at + inner + edge : at + tokens]


def back(inner_parts, outer_parts, *others):
    count, inner, width = inner_parts[0].shape
    outer = outer_parts[0].shape[1]
    bins = BACK_BINS
    tokens = inner + outer
    whole = pl.BlockSpec(memory_space=pltpu.VMEM)
    return pl.pallas_call(
        back_kernel,
        grid_spec=pltpu.PrefetchScalarGridSpec(
            num_scalar_prefetch=0,
            grid=(count // bins,),
            in_specs=[whole] * (6 + len(others)),
            out_specs=by_bin((bins, 1, tokens, width)),
            scratch_shapes=[
                pltpu.VMEM((tokens, width), jnp.float32),
                pltpu.VMEM((bins * tokens, width), jnp.bfloat16),
                pltpu.VMEM(others[5].shape, jnp.bfloat16),
            ],
        ),
        out_shape=jax.ShapeDtypeStruct((count, 1, tokens, width), jnp.bfloat16),
        name="back",
        compiler_params=pltpu.CompilerParams(vmem_limit_bytes=32 << 20),
    )(*inner_parts, *outer_parts, *others)


def prefix_kernel(slots, decay, result):
    peers, _, _ = slots.shape
    bins = decay.shape[0] // peers
    before = jnp.zeros(slots.shape[1:], jnp.float32)
    for k in range(peers):
        result[k] = before.astype(jnp.bfloat16)
        rate = decay[k * bins : (k + 1) * bins, :]
        rate = rate[0:8] * rate[8:16]
        for shift in (4, 2, 1):
            rate = rate * pltpu.roll(rate, shift, 0)
        before = rate[0:1] * before + slots[k].astype(jnp.float32)


def prefix(slots, decay):
    return pl.pallas_call(
        prefix_kernel,
        in_specs=[pl.BlockSpec(memory_space=pltpu.VMEM)] * 2,
        out_specs=pl.BlockSpec(memory_space=pltpu.VMEM),
        out_shape=jax.ShapeDtypeStruct(slots.shape, slots.dtype),
        name="prefix",
        compiler_params=pltpu.CompilerParams(vmem_limit_bytes=4 << 20),
    )(slots, decay)


def local(
    events, mix_weight, gain_in, in_weight, out_weight, skip_gain, feedforward_norm_gain,
    gate_weight, up_weight, down_weight, decay,
):
    _, _, tokens_dev, width = events.shape
    count = lax.axis_size("space")
    peers = lax.axis_size("tm")
    where = lax.axis_index("tm").astype(jnp.int32).reshape(1)
    odd = ((lax.axis_index("space") + BCOLS // 2) % 2).astype(jnp.int32).reshape(1)
    gain_row, skip_row = gain_in.reshape(1, width), skip_gain.reshape(1, width)
    near_edge, far_edge, first_row, last_row, held, *shared = pack(
        where, odd, events, mix_weight, gain_row, in_weight, decay
    )
    far = lax.ppermute(far_edge, "space", neighbour_pairs(count, lambda c: (0, 1 if c % 2 else -1)))
    near = lax.ppermute(near_edge, "space", neighbour_pairs(count, lambda c: (0, -1 if c % 2 else 1)))
    down, up = rim(odd, near, far, first_row, last_row)
    top = lax.ppermute(down, "space", neighbour_pairs(count, lambda c: (1, 0)))
    bottom = lax.ppermute(up, "space", neighbour_pairs(count, lambda c: (-1, 0)))
    *inner_parts, end_in = front(INNER, False, odd, held, near, far, (), *shared, None)
    *outer_parts, ends = front(OUTER, True, odd, held, near, far, (top, bottom), *shared, end_in)
    slots = lax.all_to_all(ends.reshape(peers, tokens_dev // peers, width), "tm", 0, 0)
    entering = lax.all_to_all(prefix(slots, decay), "tm", 0, 0).reshape(tokens_dev, width)
    return back(
        inner_parts, outer_parts, entering, shared[2], out_weight, skip_row,
        feedforward_norm_gain.reshape(1, width), gate_weight, up_weight, down_weight,
    )


def solution(mesh):
    return jax.shard_map(
        local,
        mesh=mesh,
        in_specs=(P("tm", "space", None, None), P(), P(), P(), P(), P(), P(), P(), P(), P(), P()),
        out_specs=P("tm", "space", None, None),
        check_vma=False,
    )
```
